32 devices in a mesh: rep: 16 (over z, y, core), fsdp: 2 (over x).
Axes of the slice: x: 2, y: 2, z: 4, core: 2. Of those that a mesh axis runs over, the one named last changes fastest.
Arguments:
- activations: bfloat16 [16, 1024, 1600], P('rep', 'fsdp'), may hold values from -6 to 6
- segments: int32 [16, 1024], P('rep'), may hold values from 0 to 4, never falling along the last dimension, each value on 1 to 512 neighbouring positions
- attend_gain: bfloat16 [1600], P('fsdp'), may hold values from 0.5 to 1.5
- attend_shift: bfloat16 [1600], P('fsdp'), may hold values from -3 to 3
- input_weight: bfloat16 [1600, 4800], P('fsdp'), may hold values from -0.15625 to 0.15625
- input_bias: bfloat16 [3200], P('fsdp'), may hold values from -3 to 3
- output_weight: bfloat16 [1600, 1600], P('fsdp'), may hold values from -0.625 to 0.625
- output_bias: bfloat16 [1600], P('fsdp'), may hold values from -3 to 3
- dense_gain: bfloat16 [1600], P('fsdp'), may hold values from 0.5 to 1.5
- dense_shift: bfloat16 [1600], P('fsdp'), may hold values from -3 to 3
- expand_weight: bfloat16 [1600, 6400], P('fsdp'), may hold values from -0.15625 to 0.15625
- expand_bias: bfloat16 [6400], P('fsdp'), may hold values from -3 to 3
- reduce_weight: bfloat16 [6400, 1600], P('fsdp'), may hold values from -0.078125 to 0.078125
- reduce_bias: bfloat16 [1600], P('fsdp'), may hold values from -3 to 3
- cotangent: bfloat16 [16, 1024, 1600], P('rep', 'fsdp'), may hold values from -6 to 6
Outputs:
- outputs: bfloat16 [16, 1024, 1600], P('rep', 'fsdp')
- activations_grad: bfloat16 [16, 1024, 1600], P('rep', 'fsdp')
- attend_gain_grad: float32 [1600], P('fsdp')
- attend_shift_grad: float32 [1600], P('fsdp')
- input_weight_grad: float32 [1600, 4800], P('fsdp', 'rep')
- input_bias_grad: float32 [3200], P('fsdp')
- output_weight_grad: float32 [1600, 1600], P('fsdp', 'rep')
- output_bias_grad: float32 [1600], P('fsdp')
- dense_gain_grad: float32 [1600], P('fsdp')
- dense_shift_grad: float32 [1600], P('fsdp')
- expand_weight_grad: float32 [1600, 6400], P('fsdp', 'rep')
- expand_bias_grad: float32 [6400], P('fsdp')
- reduce_weight_grad: float32 [6400, 1600], P('fsdp', 'rep')
- reduce_bias_grad: float32 [1600], P('fsdp')
The draws below stay inside these ranges and needn't reach their ends.
Inputs may be any that keep to these rules, and one draw needn't show every extreme that they name: `segments`: along each group the ids never fall and each of the 5 ids occurs; id 0 is the group's prompt, the others its continuations.
All inputs are finite; a program needn't handle non-finite values.
Results may differ from the reference program's by a relative error of at most 0.018.
Values may be sent and summed in bfloat16 or wider, within the bound.
A program may use at most 384 MiB of HBM per device.

```python
import math
import jax
import jax.numpy as jnp
import numpy as np
from jax import lax

D = 1600
HEADS = 25
HEAD_DIM = 64
FF = 6400
NSEG = 5
GROUP = 1024
MOST = 512
GROUPS = 16


def spiked(array, stream_key, source, target, parts, factor):
    owner, partner = [(jnp.arange(array.shape[dim]) // (array.shape[dim] // parts)).reshape([-1 if axis == dim else 1 for axis in range(array.ndim)]) for dim in (source, target)]
    chosen = jax.random.permutation(stream_key, parts)[partner]
    strong = (owner == chosen) | (owner == (partner + parts // 2) % parts)
    return jnp.where(strong, factor * array, array)


def levels(key, extent, pieces, least, top_value):
    level, own = 1.0, jax.random.fold_in(key, 6)
    for dim, parts in pieces:
        draws = jnp.exp(jax.random.uniform(jax.random.fold_in(own, dim), (parts,), jnp.float32, least / len(pieces), top_value / len(pieces)))
        level = level * jnp.repeat(draws, extent[dim] // parts).reshape([-1 if axis == dim else 1 for axis in range(len(extent))])
    return level


def length_profile(number_of, total, limit, skew):
    weights = [(1 << 20) // math.isqrt(rank ** skew) + 1 for rank in range(2, number_of + 1)]
    rest, counts = total - limit - (number_of - 1), [1] * (number_of - 1)
    while rest > 0:
        candidates = [i for i in range(number_of - 1) if counts[i] < limit]
        whole, left = sum([weights[i] for i in candidates]), rest
        for i in candidates:
            more = min(limit - counts[i], max(1, left * weights[i] // whole), rest)
            counts[i] = counts[i] + more
            rest = rest - more
    return np.array([limit] + counts)


def ragged_sizes(own_key, amount, total, most, slope):
    if amount == 2:
        one = jax.random.randint(own_key, (), max(1, total - most), min(most, total - 1) + 1)
        return jnp.stack([one, total - one])
    lengths = jnp.asarray(length_profile(amount, total, most, slope), jnp.int32)
    couples = (amount - 1) // 2
    donor, sink = lengths[1:1 + 2 * couples:2], lengths[2:2 + 2 * couples:2]
    margin = jnp.minimum(donor - 1, most - sink)
    passed = jax.random.randint(jax.random.fold_in(own_key, 1), (couples,), 0, 1 << 20) % (margin + 1)
    lengths = lengths.at[1:1 + 2 * couples:2].set(donor - passed).at[2:2 + 2 * couples:2].set(sink + passed)
    return lengths[jax.random.permutation(jax.random.fold_in(own_key, 2), amount)]


def bell_draw(rng, dims, scale, reach, shards=(), held_as=jnp.bfloat16):
    level = levels(rng, dims, shards, -0.22, 0.18) if shards else 1.0
    values = jax.random.normal(rng, dims, jnp.float32) * scale * level
    return jnp.minimum(jnp.maximum(values, -reach), reach).astype(held_as)


def heavy_noise(key, shape, width, limit, split, heavy, kind=jnp.bfloat16):
    entries = width * jax.random.normal(key, shape, jnp.float32)
    if split:
        entries = entries * levels(key, shape, split, -0.22, 0.18)
    return jnp.clip(spiked(entries, jax.random.fold_in(key, 3), *heavy), -limit, limit).astype(kind)


def setup_inputs(seed: int = 0) -> dict:
    keys = jax.random.split(jax.random.key(seed), 16)
    activations = bell_draw(keys[0], (GROUPS, GROUP, D), 1.0, 6.0, ((0, 16), (1, 2)))
    segments = jax.vmap(lambda own: jnp.searchsorted(jnp.cumsum(ragged_sizes(own, NSEG, GROUP, MOST, 0)), jnp.arange(GROUP), side="right"))(jax.random.split(keys[1], GROUPS)).reshape((GROUPS, GROUP)).astype(jnp.int32)
    attend_gain = jnp.clip(1.0 + 0.1 * jax.random.normal(keys[2], (D,), jnp.float32), 0.5, 1.5).astype(jnp.bfloat16)
    attend_shift = bell_draw(keys[3], (D,), 0.5, 3.0, ((0, 2),))
    input_weight = bell_draw(keys[4], (D, 3 * D), D ** -0.5, 0.15625, ((0, 2),))
    input_bias = bell_draw(keys[5], (2 * D,), 0.5, 3.0, ((0, 2),))
    output_weight = bell_draw(keys[6], (D, D), (D // 16) ** -0.5, 0.625, ((0, 2),))
    output_bias = bell_draw(keys[7], (D,), 0.5, 3.0, ((0, 2),))
    dense_gain = jnp.clip(1.0 + 0.1 * jax.random.normal(keys[8], (D,), jnp.float32), 0.5, 1.5).astype(jnp.bfloat16)
    dense_shift = bell_draw(keys[9], (D,), 0.5, 3.0, ((0, 2),))
    expand_weight = bell_draw(keys[10], (D, FF), D ** -0.5, 0.15625, ((0, 2),))
    expand_bias = bell_draw(keys[11], (FF,), 0.5, 3.0, ((0, 2),))
    reduce_weight = bell_draw(keys[12], (FF, D), FF ** -0.5, 0.078125, ((0, 2),))
    reduce_bias = bell_draw(keys[13], (D,), 0.5, 3.0, ((0, 2),))
    cotangent = heavy_noise(keys[14], (GROUPS, GROUP, D), 1.0, 6.0, ((0, 16), (1, 2)), (0, 2, 16, 2.0))
    return dict(activations=activations, segments=segments, attend_gain=attend_gain, attend_shift=attend_shift, input_weight=input_weight, input_bias=input_bias, output_weight=output_weight, output_bias=output_bias, dense_gain=dense_gain, dense_shift=dense_shift, expand_weight=expand_weight, expand_bias=expand_bias, reduce_weight=reduce_weight, reduce_bias=reduce_bias, cotangent=cotangent)


norm_eps = 1e-05
masked_score = -1e+30

@jax.custom_vjp
def low(v):
    return lax.optimization_barrier(v.astype(jnp.bfloat16)).astype(jnp.float32)

@jax.custom_vjp
def low_back(v):
    return v

def low_keep(v):
    return (low(v), None)

def low_pass(kept, grad):
    return (grad,)

def back_keep(v):
    return (v, None)

def back_low(kept, grad):
    return (low(grad),)
low.defvjp(low_keep, low_pass)
low_back.defvjp(back_keep, back_low)

def both_ways(values):
    return low(low_back(values))

def product(left, right):
    return jnp.dot(left, right, precision=lax.Precision.HIGHEST, preferred_element_type=jnp.float32)

def layer_norm(values, gain, shift):
    average = lax.optimization_barrier(jnp.mean(values, axis=-1, keepdims=True))
    centered = values - average
    variance = lax.optimization_barrier(jnp.mean(centered * centered, axis=-1, keepdims=True))
    return centered * lax.rsqrt(variance + norm_eps) * gain + shift

def allowed_pairs(segment_row):
    position = jnp.arange(segment_row.shape[0], dtype=jnp.int32)
    earlier = position[None, :] <= position[:, None]
    shared = (segment_row[None, :] == 0) | (segment_row[None, :] == segment_row[:, None])
    return earlier & shared

def group_forward(params, group_tokens, segment_row):
    attend_gain, attend_shift, input_weight, input_bias, output_weight, output_bias, dense_gain, dense_shift, expand_weight, expand_bias, reduce_weight, reduce_bias = params
    row_total = group_tokens.shape[0]
    normed = low(layer_norm(group_tokens, attend_gain, attend_shift))
    projected = product(normed, input_weight)
    queries = both_ways(projected[:, :D] + input_bias[:D])
    all_keys = both_ways(projected[:, D:2 * D])
    all_values = both_ways(projected[:, 2 * D:] + input_bias[D:])
    query_heads = queries.reshape(row_total, HEADS, HEAD_DIM)
    key_heads = all_keys.reshape(row_total, HEADS, HEAD_DIM)
    value_heads = all_values.reshape(row_total, HEADS, HEAD_DIM)
    scores = jnp.einsum('qhd,khd->hqk', query_heads, key_heads, precision=lax.Precision.HIGHEST) * HEAD_DIM ** (-0.5)
    scores = low_back(scores)
    masked = jnp.where(allowed_pairs(segment_row)[None], scores, masked_score)
    largest = lax.optimization_barrier(jnp.max(masked, axis=-1, keepdims=True))
    exponent = jnp.exp(masked - largest)
    probabilities = low(exponent / lax.optimization_barrier(jnp.sum(exponent, axis=-1, keepdims=True)))
    context = jnp.einsum('hqk,khd->qhd', probabilities, value_heads, precision=lax.Precision.HIGHEST)
    context = both_ways(context.reshape(row_total, D))
    attended = low_back(product(context, output_weight) + output_bias)
    middle = group_tokens + attended
    dense_in = low(layer_norm(middle, dense_gain, dense_shift))
    expanded = low_back(product(dense_in, expand_weight) + expand_bias)
    activated = low(jax.nn.gelu(expanded, approximate=True))
    reduced = low_back(product(activated, reduce_weight) + reduce_bias)
    return middle + reduced

def reference(activations, segments, attend_gain, attend_shift, input_weight, input_bias, output_weight, output_bias, dense_gain, dense_shift, expand_weight, expand_bias, reduce_weight, reduce_bias, cotangent):
    params = tuple((weight.astype(jnp.float32) for weight in (attend_gain, attend_shift, input_weight, input_bias, output_weight, output_bias, dense_gain, dense_shift, expand_weight, expand_bias, reduce_weight, reduce_bias)))

    def forward(weights, tokens):

        def one_group(group_pair):
            return group_forward(weights, group_pair[0], group_pair[1])
        return lax.map(jax.checkpoint(one_group), (tokens, segments))
    outputs, pullback = jax.vjp(forward, params, activations.astype(jnp.float32))
    weight_grads, input_grad = pullback(cotangent.astype(jnp.float32))
    return (outputs.astype(jnp.bfloat16), input_grad.astype(jnp.bfloat16), weight_grads[0], weight_grads[1], weight_grads[2], weight_grads[3], weight_grads[4], weight_grads[5], weight_grads[6], weight_grads[7], weight_grads[8], weight_grads[9], weight_grads[10], weight_grads[11])
```

```python
import functools

import jax
import jax.numpy as jnp
from jax import lax
from jax.experimental import pallas as pl
from jax.experimental.pallas import tpu as pltpu
from jax.sharding import PartitionSpec as P

HEADS = 25
HEAD_DIM = 64
LANES = 128
norm_eps = 1e-05
masked_score = -1e30
score_scale = HEAD_DIM ** (-0.5)
brain = jnp.bfloat16
floating = jnp.float32


def nt(a, b):
    return lax.dot_general(a, b, (((1,), (1,)), ((), ())), preferred_element_type=floating)


def nn(a, b):
    return lax.dot_general(a, b, (((1,), (0,)), ((), ())), preferred_element_type=floating)


def fill_bias(segc_ref, segr_ref, bias_ref, block):
    total = segr_ref.shape[1]
    for qi in range(total // block):
        rows = (qi + 1) * block
        seg_k = segc_ref[0:rows, :]
        seg_q = segr_ref[:, qi * block : (qi + 1) * block]
        pos_k = lax.broadcasted_iota(jnp.int32, (rows, block), 0)
        pos_q = lax.broadcasted_iota(jnp.int32, (rows, block), 1) + qi * block
        seen = (pos_k <= pos_q) & ((seg_k == 0) | (seg_k == seg_q))
        bias_ref[0:rows, qi * block : (qi + 1) * block] = jnp.where(seen, 0.0, masked_score)


def half_lanes(value, e):
    lane = lax.broadcasted_iota(jnp.int32, value.shape, 1)
    return jnp.where((lane // HEAD_DIM) == e, value, jnp.zeros_like(value))


def attend_kernel(meta, segc_ref, segr_ref, x_ref, o_ref, lse_ref, bias_ref, q_ref, k_ref, vt_ref, ot_ref, *, block, own):
    total = x_ref.shape[0]
    blocks = total // block
    me = meta[0]
    p = pl.program_id(0)

    @pl.when(p == 0)
    def _():
        fill_bias(segc_ref, segr_ref, bias_ref, block)

    def where_is(b):
        return pl.multiple_of(jnp.bitwise_xor(b, me * (own // block)) * block, block)

    for b in range(blocks):
        rows = pl.ds(where_is(b), block)
        q_ref[b * block : (b + 1) * block, :] = x_ref[rows, 0:LANES] * jnp.asarray(score_scale, brain)
        k_ref[b * block : (b + 1) * block, :] = x_ref[rows, LANES : 2 * LANES]
        vt_ref[:, b * block : (b + 1) * block] = x_ref[rows, 2 * LANES : 3 * LANES].T
    for e in range(2):
        valid = meta[1 + 2 * p + e] == 1
        feats = slice(e * HEAD_DIM, (e + 1) * HEAD_DIM)

        @pl.when(valid)
        def _():
            for qi in range(blocks):
                cols = slice(qi * block, (qi + 1) * block)
                keys = (qi + 1) * block
                query = half_lanes(q_ref[cols, :], e)
                scores = nt(k_ref[0:keys, :], query) + bias_ref[0:keys, cols]
                largest = jnp.max(scores, axis=0, keepdims=True)
                exponent = jnp.exp(scores - largest)
                denominator = jnp.sum(exponent, axis=0, keepdims=True)
                context = nn(vt_ref[feats, 0:keys], exponent.astype(brain)) / denominator
                ot_ref[feats, cols] = context
                lse_ref[0, e : e + 1, cols] = largest + jnp.log(denominator)

        @pl.when(jnp.logical_not(valid))
        def _():
            ot_ref[feats, :] = jnp.zeros((HEAD_DIM, total), floating)
            lse_ref[0, e : e + 1, :] = jnp.zeros((1, total), floating)

    for b in range(blocks):
        o_ref[pl.ds(where_is(b), block), :] = ot_ref[:, b * block : (b + 1) * block].T.astype(brain)


def attend_back_kernel(
    meta, segc_ref, segr_ref, x_ref, o_ref, do_ref, lse_ref, dx_ref,
    bias_ref, q_ref, k_ref, v_ref, d_ref, kt_ref, delta_ref, dqt_ref, dk_ref, dv_ref, *, block, own,
):
    total = x_ref.shape[0]
    blocks = total // block
    me = meta[0]
    p = pl.program_id(0)

    @pl.when(p == 0)
    def _():
        fill_bias(segc_ref, segr_ref, bias_ref, block)

    def where_is(b):
        return pl.multiple_of(jnp.bitwise_xor(b, me * (own // block)) * block, block)

    for b in range(blocks):
        rows = pl.ds(where_is(b), block)
        here = slice(b * block, (b + 1) * block)
        q_ref[here, :] = x_ref[rows, 0:LANES] * jnp.asarray(score_scale, brain)
        key = x_ref[rows, LANES : 2 * LANES]
        k_ref[here, :] = key
        kt_ref[:, here] = (key * jnp.asarray(score_scale, brain)).T
        v_ref[here, :] = x_ref[rows, 2 * LANES : 3 * LANES]
        grad = do_ref[rows, :]
        d_ref[here, :] = grad
        both = (grad.astype(floating) * o_ref[rows, :].astype(floating)).T
        delta_ref[0:1, here] = jnp.sum(both[0:HEAD_DIM, :], axis=0, keepdims=True)
        delta_ref[1:2, here] = jnp.sum(both[HEAD_DIM:, :], axis=0, keepdims=True)
    dk_ref[...] = jnp.zeros_like(dk_ref)
    dv_ref[...] = jnp.zeros_like(dv_ref)
    for e in range(2):
        valid = meta[1 + 2 * p + e] == 1
        feats = slice(e * HEAD_DIM, (e + 1) * HEAD_DIM)

        @pl.when(valid)
        def _():
            for qi in range(blocks):
                cols = slice(qi * block, (qi + 1) * block)
                keys = (qi + 1) * block
                query = half_lanes(q_ref[cols, :], e)
                grad = half_lanes(d_ref[cols, :], e)
                scores = nt(k_ref[0:keys, :], query) + bias_ref[0:keys, cols]
                prob = jnp.exp(scores - lse_ref[0, e : e + 1, cols])
                prob_grad = nt(v_ref[0:keys, :], grad)
                score_grad = (prob * (prob_grad - delta_ref[e : e + 1, cols])).astype(brain)
                dqt_ref[feats, cols] = nn(kt_ref[feats, 0:keys], score_grad)
                dv_ref[0:keys, :] += nn(prob.astype(brain), grad)
                dk_ref[0:keys, :] += nn(score_grad, query)

        @pl.when(jnp.logical_not(valid))
        def _():
            dqt_ref[feats, :] = jnp.zeros((HEAD_DIM, total), floating)

    for b in range(blocks):
        rows = pl.ds(where_is(b), block)
        here = slice(b * block, (b + 1) * block)
        dx_ref[rows, 0:LANES] = dqt_ref[:, here].T.astype(brain)
        dx_ref[rows, LANES : 2 * LANES] = dk_ref[here, :].astype(brain)
        dx_ref[rows, 2 * LANES : 3 * LANES] = dv_ref[here, :].astype(brain)


def attend(meta, segments, mixed, own):
    total, width = mixed.shape
    pairs = width // (3 * LANES)
    block = min(own, 256)
    fixed = lambda p, m: (0, 0)
    macs = total * total * LANES * pairs * 2
    return pl.pallas_call(
        functools.partial(attend_kernel, block=block, own=own),
        grid_spec=pltpu.PrefetchScalarGridSpec(
            num_scalar_prefetch=1,
            grid=(pairs,),
            in_specs=[
                pl.BlockSpec((total, 1), fixed),
                pl.BlockSpec((1, total), fixed),
                pl.BlockSpec((total, 3 * LANES), lambda p, m: (0, p)),
            ],
            out_specs=[
                pl.BlockSpec((total, LANES), lambda p, m: (0, p)),
                pl.BlockSpec((1, 8, total), lambda p, m: (p, 0, 0)),
            ],
            scratch_shapes=[
                pltpu.VMEM((total, total), floating),
                pltpu.VMEM((total, LANES), brain),
                pltpu.VMEM((total, LANES), brain),
                pltpu.VMEM((LANES, total), brain),
                pltpu.VMEM((LANES, total), floating),
            ],
        ),
        out_shape=[
            jax.ShapeDtypeStruct((total, pairs * LANES), brain),
            jax.ShapeDtypeStruct((pairs, 8, total), floating),
        ],
        compiler_params=pltpu.CompilerParams(vmem_limit_bytes=40 * 2**20),
        cost_estimate=pl.CostEstimate(
            flops=2 * macs, bytes_accessed=total * width * 3, transcendentals=total * total * pairs
        ),
        name="attend",
    )(meta, segments.reshape(total, 1), segments.reshape(1, total), mixed)


def attend_back(meta, segments, mixed, context, grad, log_total, own):
    total, width = mixed.shape
    pairs = width // (3 * LANES)
    block = min(own, 256)
    fixed = lambda p, m: (0, 0)
    macs = total * total * LANES * pairs * 5
    return pl.pallas_call(
        functools.partial(attend_back_kernel, block=block, own=own),
        grid_spec=pltpu.PrefetchScalarGridSpec(
            num_scalar_prefetch=1,
            grid=(pairs,),
            in_specs=[
                pl.BlockSpec((total, 1), fixed),
                pl.BlockSpec((1, total), fixed),
                pl.BlockSpec((total, 3 * LANES), lambda p, m: (0, p)),
                pl.BlockSpec((total, LANES), lambda p, m: (0, p)),
                pl.BlockSpec((total, LANES), lambda p, m: (0, p)),
                pl.BlockSpec((1, 8, total), lambda p, m: (p, 0, 0)),
            ],
            out_specs=pl.BlockSpec((total, 3 * LANES), lambda p, m: (0, p)),
            scratch_shapes=[
                pltpu.VMEM((total, total), floating),
                pltpu.VMEM((total, LANES), brain),
                pltpu.VMEM((total, LANES), brain),
                pltpu.VMEM((total, LANES), brain),
                pltpu.VMEM((total, LANES), brain),
                pltpu.VMEM((LANES, total), brain),
                pltpu.VMEM((8, total), floating),
                pltpu.VMEM((LANES, total), floating),
                pltpu.VMEM((total, LANES), floating),
                pltpu.VMEM((total, LANES), floating),
            ],
        ),
        out_shape=jax.ShapeDtypeStruct((total, width), brain),
        compiler_params=pltpu.CompilerParams(vmem_limit_bytes=40 * 2**20),
        cost_estimate=pl.CostEstimate(
            flops=2 * macs, bytes_accessed=total * width * 6, transcendentals=total * total * pairs
        ),
        name="attend_back",
    )(meta, segments.reshape(total, 1), segments.reshape(1, total), mixed, context, grad, log_total)


def stats(values):
    average = jnp.mean(values, axis=-1, keepdims=True)
    centered = values - average
    variance = jnp.mean(centered * centered, axis=-1, keepdims=True)
    return average, lax.rsqrt(variance + norm_eps)


def norm_back(values, average, inverse, gain, grad):
    unit = (values - average) * inverse
    scaled = grad * gain
    middle = jnp.mean(scaled, axis=-1, keepdims=True)
    along = jnp.mean(scaled * unit, axis=-1, keepdims=True)
    return inverse * (scaled - middle - unit * along), jnp.sum(grad * unit, axis=0), jnp.sum(grad, axis=0)


def tn(a, b):
    return lax.dot_general(a, b, (((0,), (0,)), ((), ())), preferred_element_type=floating)


def local(
    devices, reps,
    activations, segments, attend_gain, attend_shift, input_weight, input_bias, output_weight, output_bias,
    dense_gain, dense_shift, expand_weight, expand_bias, reduce_weight, reduce_bias, cotangent,
):
    me = lax.axis_index("fsdp")
    rep = lax.axis_index("rep")
    core = rep & 1
    tokens = activations[0].astype(floating)
    own, width = tokens.shape
    total = own * devices
    hidden = expand_weight.shape[1]
    hidden_own = hidden // devices
    all_pairs = -(-HEADS // 2)
    heads_own = -(-HEADS // devices)
    pairs = (heads_own + 1) // 2
    starts = [min(heads_own * f // 2, all_pairs - pairs) for f in range(devices)]
    start_of = lambda f: jnp.minimum(heads_own * f // 2, all_pairs - pairs)
    slot_heads = 2 * start_of(me) + jnp.arange(2 * pairs, dtype=jnp.int32)
    valid = (slot_heads >= heads_own * me) & (slot_heads < jnp.minimum(heads_own * (me + 1), HEADS))
    meta = jnp.concatenate([me[None].astype(jnp.int32), valid.astype(jnp.int32)])

    def fswap(value, d=1):
        return lax.ppermute(value, "fsdp", [(i, i ^ d) for i in range(devices)])

    def rswap(value, bit):
        return lax.ppermute(value, "rep", [(i, i ^ bit) for i in range(reps)])

    def gather_tokens(value):
        return jnp.concatenate([value] + [fswap(value, d) for d in range(1, devices)], axis=0)

    def in_order(parts):
        if devices == 2:
            return [jnp.where(me == f, parts[0], parts[1]) for f in range(2)]
        stacked = jnp.stack(parts)
        return [lax.dynamic_index_in_dim(stacked, me ^ f, 0, keepdims=False) for f in range(devices)]

    def fetch(weight, columns):
        rows = weight.shape[0]
        half = rows // 2
        mine = columns(weight, me)
        shape = (devices, 2, half) + mine.shape[1:]
        result = jnp.broadcast_to(mine.reshape((1, 2, half) + mine.shape[1:]), shape)
        part = lax.dynamic_slice_in_dim(weight, core * half, half, 0)
        zero = [0] * (mine.ndim - 1)
        for d in range(1, devices):
            first = fswap(columns(part, me ^ d), d)
            second = rswap(first, 1)
            result = lax.dynamic_update_slice(result, first[None, None], [me ^ d, core, 0] + zero)
            result = lax.dynamic_update_slice(result, second[None, None], [me ^ d, core ^ 1, 0] + zero)
        return result.reshape((devices * rows,) + mine.shape[1:])

    def pair_columns(weight, f):
        rows = weight.shape[0]
        padded = jnp.pad(weight.reshape(rows, 3, width), ((0, 0), (0, 0), (0, all_pairs * LANES - width)))
        padded = padded.reshape(rows, 3, all_pairs, LANES)
        taken = lax.dynamic_slice_in_dim(padded, start_of(f), pairs, 2)
        return taken.transpose(0, 2, 1, 3).reshape(rows, pairs * 3 * LANES)

    def hidden_columns(weight, f):
        return lax.dynamic_slice_in_dim(weight, f * hidden_own, hidden_own, 1)

    small = jnp.concatenate(
        [attend_gain, attend_shift, output_bias, dense_gain, dense_shift, reduce_bias, input_bias]
    )
    gathered = lax.all_gather(small, "fsdp", axis=0, tiled=False)
    piece = attend_gain.shape[0]
    full = [gathered[:, i * piece : (i + 1) * piece].reshape(-1).astype(floating) for i in range(6)]
    first_gain, first_shift, after_bias, second_gain, second_shift, last_bias = full
    mixing_bias = gathered[:, 6 * piece :].reshape(-1)
    three_bias = jnp.concatenate([mixing_bias[:width], jnp.zeros((width,), brain), mixing_bias[width:]])
    own_bias = pair_columns(three_bias[None], me).astype(floating)

    average, inverse = stats(tokens)
    normed = ((tokens - average) * inverse * first_gain + first_shift).astype(brain)
    input_own = fetch(input_weight, pair_columns)
    normed_all = gather_tokens(normed)
    mixed = (nn(normed_all, input_own) + own_bias).astype(brain)
    context_all, log_total = attend(meta, segments[0], mixed, own)

    def place(parts):
        ordered = in_order(parts)
        result = 0
        for f in range(devices):
            before = starts[f] * LANES
            after = all_pairs * LANES - before - pairs * LANES
            result = result + jnp.pad(ordered[f], ((0, 0), (before, after)))
        return result[:, :width]

    context = place(
        [context_all[:own]] + [fswap(context_all[d * own : (d + 1) * own], d) for d in range(1, devices)]
    )
    output_full = fetch(output_weight, lambda w, f: w)
    middle = tokens + (nn(context, output_full) + after_bias)

    average_2, inverse_2 = stats(middle)
    dense = ((middle - average_2) * inverse_2 * second_gain + second_shift).astype(brain)
    expand_own = fetch(expand_weight, hidden_columns)
    incoming_low = cotangent[0]
    incoming = incoming_low.astype(floating)
    incoming_all = gather_tokens(incoming_low)
    activated_grad = nt(incoming_all, reduce_weight).astype(brain)
    dense_all = gather_tokens(dense)
    expanded = nn(dense_all, expand_own) + expand_bias.astype(floating)
    activated, gelu_pull = jax.vjp(lambda v: jax.nn.gelu(v, approximate=True), expanded)
    activated = activated.astype(brain)
    expanded_grad = gelu_pull(activated_grad.astype(floating))[0].astype(brain)

    def scatter_tokens(left, right, product):
        result = product(left[:own], right)
        for d in range(1, devices):
            sent = product(left[d * own : (d + 1) * own], right).astype(brain)
            result = result + fswap(sent, d).astype(floating)
        return result

    dense_bar = scatter_tokens(expanded_grad, expand_own, nt)
    outputs = (middle + (scatter_tokens(activated, reduce_weight, nn) + last_bias)).astype(brain)
    norm_grad, dense_gain_part, dense_shift_part = norm_back(middle, average_2, inverse_2, second_gain, dense_bar)
    middle_grad = incoming + norm_grad
    attended_low = middle_grad.astype(brain)

    def halve(value, axis, bit):
        mine = (rep // bit) & 1
        sent = rswap(lax.dynamic_index_in_dim(value, mine ^ 1, axis, keepdims=False), bit)
        kept = lax.dynamic_index_in_dim(value, mine, axis, keepdims=False)
        return (kept.astype(floating) + sent.astype(floating)).astype(brain)

    def bits_of(count):
        return [1 << i for i in range(count.bit_length() - 1)]

    def halve_all(value, bits):
        low = bits[0]
        for bit in bits:
            value = value.reshape((value.shape[0] // 2, 2) + value.shape[1:])
            value = halve(value, 1, bit)
        return value[0]

    def columns_of(value, d):
        part = value.shape[-1] // devices
        return lax.dynamic_slice_in_dim(value, (me ^ d) * part, part, value.ndim - 1)

    reduce_grad = tn(incoming_all, activated).astype(brain).reshape(reps, width // reps, hidden_own)
    reduce_grad = halve_all(reduce_grad, bits_of(reps)).astype(floating).T

    local_blocks = reps // devices
    expand_grad = tn(expanded_grad, dense_all).astype(brain).reshape(local_blocks, hidden // reps, width)
    expand_grad = halve_all(expand_grad, bits_of(local_blocks))
    parts = [columns_of(expand_grad, 0)] + [fswap(columns_of(expand_grad, d), d) for d in range(1, devices)]
    expand_grad = jnp.stack(in_order(parts))
    expand_grad = halve_all(expand_grad, [bit * local_blocks for bit in bits_of(devices)]).astype(floating).T

    context_bar = nt(attended_low, output_full).astype(brain)
    context_bar_pad = jnp.pad(context_bar, ((0, 0), (0, all_pairs * LANES - width)))
    take_pairs = lambda f: lax.dynamic_slice_in_dim(context_bar_pad, start_of(f) * LANES, pairs * LANES, 1)
    context_bar_all = jnp.concatenate(
        [take_pairs(me)] + [fswap(take_pairs(me ^ d), d) for d in range(1, devices)], axis=0
    )
    output_grad = tn(attended_low, context).astype(brain).reshape(reps, width // reps, width)
    output_grad = halve_all(output_grad, bits_of(reps))
    output_sum = columns_of(output_grad, 0).astype(floating)
    for d in range(1, devices):
        output_sum = output_sum + fswap(columns_of(output_grad, d), d).astype(floating)
    output_grad = output_sum.T

    mixed_bar = attend_back(meta, segments[0], mixed, context_all, context_bar_all, log_total, own)
    normed_bar = scatter_tokens(mixed_bar, input_own, nt)
    token_grad, attend_gain_part, attend_shift_part = norm_back(tokens, average, inverse, first_gain, normed_bar)
    input_grads = (middle_grad + token_grad).astype(brain)

    quarter = width // devices // 2
    normed_quarters = normed_all.reshape(total, devices, 2, quarter)
    take = lambda c: lax.dynamic_index_in_dim(normed_quarters, c, 2, keepdims=False).reshape(total, devices * quarter)
    sent = rswap(tn(take(core ^ 1), mixed_bar).astype(brain), 1)
    input_grad = (tn(take(core), mixed_bar) + sent.astype(floating)).astype(brain)
    input_grad = input_grad.reshape(devices, quarter, pairs * 3 * LANES)
    pick = lambda d: lax.dynamic_index_in_dim(input_grad, me ^ d, 0, keepdims=False)
    ordered = in_order([pick(0)] + [fswap(pick(d), d) for d in range(1, devices)])
    columns = 0
    for f in range(devices):
        shaped = ordered[f].reshape(quarter, pairs, 3, LANES)
        columns = columns + jnp.pad(shaped, ((0, 0), (starts[f], all_pairs - pairs - starts[f]), (0, 0), (0, 0)))
    columns = columns.transpose(0, 2, 1, 3).reshape(quarter, 3, all_pairs * LANES)[:, :, :width]
    columns = columns.reshape(quarter, reps // 2, 2 * 3 * width // reps).transpose(1, 0, 2)
    columns = halve_all(columns, [2 * bit for bit in bits_of(reps // 2)])
    columns = columns.reshape(quarter, 2, 3 * width // reps)
    kept = lax.dynamic_index_in_dim(columns, core, 1, keepdims=False)
    came = rswap(lax.dynamic_index_in_dim(columns, core ^ 1, 1, keepdims=False), 1)
    input_grad = jnp.concatenate([jnp.where(core == 0, kept, came), jnp.where(core == 0, came, kept)], axis=0)
    input_grad = input_grad.astype(floating)

    sums = jnp.sum(mixed_bar.astype(floating), axis=0).reshape(pairs, 3, LANES)
    bias_full = lax.dynamic_update_slice(jnp.zeros((all_pairs, 3, LANES), floating), sums, [start_of(me), 0, 0])
    bias_full = bias_full.transpose(1, 0, 2).reshape(3, all_pairs * LANES)[:, :width]
    expand_sum = lax.dynamic_update_slice(
        jnp.zeros((hidden,), floating), jnp.sum(expanded_grad.astype(floating), axis=0), [me * hidden_own]
    )
    vectors = [
        attend_gain_part, attend_shift_part, bias_full[0], bias_full[2],
        jnp.sum(attended_low.astype(floating), axis=0), dense_gain_part, dense_shift_part,
        jnp.sum(incoming, axis=0), expand_sum,
    ]
    flat = lax.psum(jnp.concatenate(vectors), ("rep", "fsdp"))

    def share(start, length):
        part = length // devices
        return lax.dynamic_slice_in_dim(flat, start + me * part, part, 0)

    w = width
    return (
        outputs[None],
        input_grads[None],
        share(0, w),
        share(w, w),
        input_grad,
        share(2 * w, 2 * w),
        output_grad,
        share(4 * w, w),
        share(5 * w, w),
        share(6 * w, w),
        expand_grad,
        share(8 * w, hidden),
        reduce_grad,
        share(7 * w, w),
    )


def solution(mesh):
    row, matrix = P("fsdp"), P("fsdp", None)
    tokens = P("rep", "fsdp", None)
    in_specs = (
        tokens, P("rep", None), row, row, matrix, row, matrix, row, row, row, matrix, row, matrix, row, tokens,
    )
    split = P("fsdp", "rep")
    out_specs = (tokens, tokens, row, row, split, row, split, row, row, row, split, row, split, row)
    return jax.shard_map(
        functools.partial(local, mesh.shape["fsdp"], mesh.shape["rep"]),
        mesh=mesh, in_specs=in_specs, out_specs=out_specs, check_vma=False,
    )
```
